32 devices in a mesh: row: 4 (over z), col: 8 (over y, x, core).
Axes of the slice: x: 2, y: 2, z: 4, core: 2. Of those that a mesh axis runs over, the one named last changes fastest.
Arguments:
- hidden_state: bfloat16 [512, 8192], P('col', 'row'), may hold values from -6 to 6
- norm_gain: float32 [8192], P('row'), may hold values from 0.5 to 1.5
- head_weight: bfloat16 [8192, 65536], P('row', 'col'), may hold values from -40 to 40
- targets: int32 [512], replicated, may hold values from 0 to 65535
- gate_act: bfloat16 [512, 26624], P(None, 'col'), may hold values from -6 to 6
- up_act: bfloat16 [512, 26624], P(None, 'col'), may hold values from -6 to 6
Outputs:
- head_grad: bfloat16 [8192, 65536], P('row', 'col')
- grad_hidden: bfloat16 [512, 8192], P('col', 'row')
- down_grad: bfloat16 [26624, 8192], P('col', 'row')
The draws below stay inside these ranges and needn't reach their ends.
All inputs are finite; a program needn't handle non-finite values.
Results may differ from the reference program's by a relative error of at most 0.024.
Values may be sent and summed in bfloat16 or wider, within the bound.
No kernel may reach another device: no remote copies, remote signals or barrier semaphores. Data moves between devices by JAX's collectives and lax.ppermute only.
A program may use at most 192 MiB of HBM per device.

```python
import math
import jax
import jax.numpy as jnp
from jax import lax

D = 8192
FF = 26624
V = 65536
TOKENS = 512


def base_hidden(key):
    inner = jax.random.fold_in(key, 11)
    return jnp.clip(jax.random.normal(jax.random.fold_in(inner, 3), (TOKENS, D), jnp.float32), -6.0, 6.0)


def draw_hidden_state(key, part):
    return base_hidden(key).astype(jnp.bfloat16)


def draw_head_weight(key, part):
    inner = jax.random.fold_in(key, 23)
    weights = jax.random.normal(jax.random.fold_in(inner, 1), (D, V), jnp.float32) * (3.0 / jnp.sqrt(float(D)))
    hidden_rows = base_hidden(key)
    chosen_tokens = jax.random.permutation(jax.random.fold_in(inner, 2), TOKENS)[:6]
    chosen_columns = jax.random.permutation(jax.random.fold_in(inner, 3), V)[:12]
    strengths = jnp.array([130.0, 131.5, 210.0, 212.0, 330.0, 332.5, 160.0, 162.0, 260.0, 261.0, 300.0, 302.5], jnp.float32)
    picked = hidden_rows[chosen_tokens[jnp.arange(12) // 2]]
    norms = jnp.sqrt(jnp.mean(picked * picked, axis=1, keepdims=True))
    columns = (picked / norms * strengths[:, None] / D).T
    weights = weights.at[:, chosen_columns].set(columns)
    return jnp.clip(weights, -40.0, 40.0).astype(jnp.bfloat16)


def set_ends(result, own_key, smallest, high):
    longest = result.shape.index(max(result.shape))
    spots = []
    for shift in (0, 1):
        where = [jax.random.randint(jax.random.fold_in(own_key, axis), (), 0, length) for axis, length in enumerate(result.shape)]
        where[longest] = (where[longest] + shift) % result.shape[longest]
        spots.append(tuple(where))
    return result.at[spots[0]].set(smallest).at[spots[1]].set(high)


def level_of(own_key, extent, pieces, least, top_value):
    def one(position, blocks):
        heights = jax.random.uniform(jax.random.fold_in(jax.random.fold_in(own_key, 6), position), (blocks,), jnp.float32, least / len(pieces), top_value / len(pieces))
        return jnp.repeat(jnp.exp(heights), extent[position] // blocks).reshape((-1,) + (1,) * (len(extent) - position - 1))

    gain = one(*pieces[0])
    for cut in pieces[1:]:
        gain = gain * one(*cut)
    return gain


def gaussian(own_key, shape, deviation, limit, cuts=(), kind=jnp.bfloat16):
    gain = level_of(own_key, shape, cuts, -0.22, 0.18) if cuts else 1.0
    result = jax.random.normal(own_key, shape, jnp.float32) * deviation * gain
    return jnp.minimum(jnp.maximum(result, -limit), limit).astype(kind)


def setup_inputs(seed: int = 0) -> dict:
    key_list = jax.random.split(jax.random.key(seed), 7)
    hidden_state = draw_hidden_state(jax.random.fold_in(key_list[6], 71), 0)
    norm_gain = jnp.clip(1.0 + 0.1 * jax.random.normal(key_list[1], (D,), jnp.float32), 0.5, 1.5)
    head_weight = draw_head_weight(jax.random.fold_in(key_list[6], 71), 0)
    targets = set_ends(jax.random.randint(key_list[3], (TOKENS,), 0, V), jax.random.fold_in(key_list[3], 1), 0, V - 1).astype(jnp.int32)
    gate_act = gaussian(key_list[4], (TOKENS, FF), 1.0, 6.0, ((1, 8),))
    up_act = gaussian(key_list[5], (TOKENS, FF), 1.0, 6.0, ((1, 8),))
    return {"hidden_state": hidden_state, "norm_gain": norm_gain, "head_weight": head_weight, "targets": targets, "gate_act": gate_act, "up_act": up_act}


def reference(hidden_state, norm_gain, head_weight, targets, gate_act, up_act):
    widened = hidden_state.astype(jnp.float32)
    scaled = (norm_gain[None, :] * widened).astype(jnp.bfloat16)
    inv_rms = 1.0 / jnp.sqrt(lax.optimization_barrier(jnp.sum(widened * widened, axis=1)) / D + 1e-05)
    logits = inv_rms[:, None] * jnp.dot(scaled, head_weight, preferred_element_type=jnp.float32)
    top_logit = lax.optimization_barrier(jnp.max(logits, axis=1))
    shifted = jnp.exp(logits - top_logit[:, None])
    exp_total = lax.optimization_barrier(jnp.sum(shifted, axis=1))
    moment = lax.optimization_barrier(jnp.sum(shifted * logits, axis=1))
    matches = targets[:, None] == jnp.arange(V, dtype=jnp.int32)[None, :]
    target_logit = lax.optimization_barrier(jnp.sum(jnp.where(matches, logits, 0.0), axis=1))
    scaled_grad = (inv_rms[:, None] * (shifted / exp_total[:, None] - matches.astype(jnp.float32))).astype(jnp.bfloat16)
    curvature = moment / exp_total - target_logit
    block_width = math.gcd(V, 4096)
    grad_blocks = scaled_grad.reshape(TOKENS, V // block_width, block_width).transpose(1, 0, 2)

    def head_block(grad_block):
        return lax.dot_general(scaled, grad_block, (((0,), (0,)), ((), ())), preferred_element_type=jnp.float32).astype(jnp.bfloat16)
    head_grad = lax.map(head_block, grad_blocks).transpose(1, 0, 2).reshape(D, V)
    feature_grad = lax.dot_general(scaled_grad, head_weight, (((1,), (1,)), ((), ())), preferred_element_type=jnp.float32)
    grad_hidden = (norm_gain[None, :] * feature_grad - widened * (inv_rms * inv_rms * curvature)[:, None] / D).astype(jnp.bfloat16)
    activation = (jax.nn.silu(gate_act.astype(jnp.float32)) * up_act.astype(jnp.float32)).astype(jnp.bfloat16)
    down_grad = lax.dot_general(activation, grad_hidden, (((0,), (0,)), ((), ())), preferred_element_type=jnp.float32).astype(jnp.bfloat16)
    return (head_grad, grad_hidden, down_grad)
```

```python
import jax
import jax.numpy as jnp
from jax import lax
from jax.sharding import PartitionSpec as P

CHUNKS = 4


def combine(left_part, right_part):
    biggest = jnp.maximum(left_part[0], right_part[0])
    left_scale = jnp.exp(left_part[0] - biggest)
    right_scale = jnp.exp(right_part[0] - biggest)
    return (
        biggest,
        left_part[1] * left_scale + right_part[1] * right_scale,
        left_part[2] * left_scale + right_part[2] * right_scale,
        left_part[3] + right_part[3],
    )


def encode(value):
    largest = jnp.maximum(jnp.max(jnp.abs(value), axis=1, keepdims=True), 1e-30)
    codes = jnp.round(value * (32767.0 / largest)).astype(jnp.int16)
    return codes, (largest * (1.0 / 32767.0))[:, 0]


def decode(codes, scale):
    return codes.astype(jnp.float32) * scale[:, None]


def over_col(stats):
    size = lax.axis_size("col")
    step = 1
    while step < size:
        packed = jnp.stack(stats)
        other = lax.ppermute(packed, "col", [(i, i ^ step) for i in range(size)])
        stats = combine(stats, tuple(other[i] for i in range(4)))
        step *= 2
    return stats


def on_device(hidden_state, norm_gain, head_weight, targets, gate_act, up_act):
    tok_col, feats = hidden_state.shape
    vocab_part = head_weight.shape[1]
    cols = lax.axis_size("col")
    rows = lax.axis_size("row")
    half = rows // 2
    row = lax.axis_index("row")
    col = lax.axis_index("col")
    all_feats = feats * rows
    tk = tok_col // CHUNKS
    tc = tk * cols
    vocab_start = col * vocab_part
    target_chunks = targets.reshape(cols, CHUNKS, tk)

    activation = (jax.nn.silu(gate_act.astype(jnp.float32)) * up_act.astype(jnp.float32)).astype(
        jnp.bfloat16
    )

    def first(k):
        gathered = lax.all_gather(hidden_state[k * tk : (k + 1) * tk], "col", axis=0, tiled=True)
        wide = gathered.astype(jnp.float32)
        scaled = (norm_gain[None, :] * wide).astype(jnp.bfloat16)
        squares = jnp.sum(wide * wide, axis=1)
        product = jnp.dot(scaled, head_weight, preferred_element_type=jnp.float32)
        return scaled, squares, product

    def reduce_rows(product, squares):
        total, sq = product, squares
        for s in range(half):
            codes, scale = encode(total)
            if s < half - 1:
                pairs = [(s, s + 1), (rows - 1 - s, rows - 2 - s)]
            else:
                pairs = [(half - 1, half), (half, half - 1)]
            got = lax.ppermute(codes, "row", pairs)
            aux = lax.ppermute(jnp.stack([scale, sq]), "row", pairs)
            total = total + decode(got, aux[0])
            sq = sq + aux[1]
        return total, sq

    def softmax_grad(total, sq, k):
        inv_rms = 1.0 / jnp.sqrt(sq / all_feats + 1e-05)
        logits = inv_rms[:, None] * total
        local_max = jnp.max(logits, axis=1)
        shifted = jnp.exp(logits - local_max[:, None])
        local_sum = jnp.sum(shifted, axis=1)
        local_moment = jnp.sum(shifted * logits, axis=1)
        mine = target_chunks[:, k].reshape(tc)
        matches = (
            mine[:, None] - vocab_start == jnp.arange(vocab_part, dtype=jnp.int32)[None, :]
        )
        local_target = jnp.sum(jnp.where(matches, logits, 0.0), axis=1)
        top, exp_total, moment, target_logit = over_col(
            (local_max, local_sum, local_moment, local_target)
        )
        probs = jnp.exp(logits - top[:, None]) / exp_total[:, None]
        grad = (inv_rms[:, None] * (probs - matches.astype(jnp.float32))).astype(jnp.bfloat16)
        curvature = moment / exp_total - target_logit
        return grad, jnp.stack([inv_rms, curvature])

    def spread_rows(grad, aux):
        for s in range(half - 2, -1, -1):
            pairs = [(s + 1, s), (rows - 2 - s, rows - 1 - s)]
            got = lax.ppermute(grad, "row", pairs)
            got_aux = lax.ppermute(aux, "row", pairs)
            here = (row == s) | (row == rows - 1 - s)
            grad = jnp.where(here, got, grad)
            aux = jnp.where(here, got_aux, aux)
        return grad, aux

    def feature(grad, aux, k):
        part = lax.dot_general(
            grad, head_weight, (((1,), (1,)), ((), ())), preferred_element_type=jnp.float32
        ).astype(jnp.bfloat16)
        feature_grad = lax.psum_scatter(part, "col", scatter_dimension=0, tiled=True).astype(
            jnp.float32
        )
        mine = lax.dynamic_slice_in_dim(aux, col * tk, tk, axis=1)
        wide = hidden_state[k * tk : (k + 1) * tk].astype(jnp.float32)
        return (
            norm_gain[None, :] * feature_grad
            - wide * (mine[0] * mine[0] * mine[1])[:, None] / all_feats
        ).astype(jnp.bfloat16)

    scaled_all, grads, hidden_grads = [], [], []
    for k in range(CHUNKS):
        scaled, squares, product = first(k)
        scaled_all.append(scaled)
        total, sq = reduce_rows(product, squares)
        grad, aux = spread_rows(*softmax_grad(total, sq, k))
        grads.append(grad)
        hidden_grads.append(feature(grad, aux, k))

    head_grad = lax.dot_general(
        jnp.concatenate(scaled_all),
        jnp.concatenate(grads),
        (((0,), (0,)), ((), ())),
        preferred_element_type=jnp.float32,
    ).astype(jnp.bfloat16)
    grad_hidden = jnp.concatenate(hidden_grads)
    down_sum = lax.dot_general(
        activation,
        lax.all_gather(grad_hidden, "col", axis=0, tiled=True),
        (((0,), (0,)), ((), ())),
        preferred_element_type=jnp.float32,
    )
    return (head_grad, grad_hidden, down_sum.astype(jnp.bfloat16))


def solution(mesh):
    in_specs = (P("col", "row"), P("row"), P("row", "col"), P(), P(None, "col"), P(None, "col"))
    out_specs = (P("row", "col"), P("col", "row"), P("col", "row"))
    return jax.shard_map(
        on_device, mesh=mesh, in_specs=in_specs, out_specs=out_specs, check_vma=False
    )
```

```python
import jax
import jax.numpy as jnp
from jax import lax
from jax.experimental import pallas as pl
from jax.experimental.pallas import tpu as pltpu
from jax.sharding import PartitionSpec as P

CHUNKS = 4
HALVES = 2
LANES = 128
SQ = 8

f32 = jnp.float32
bf16 = jnp.bfloat16
ANY = pl.BlockSpec(memory_space=pl.ANY)


def sds(shape, dtype):
    return jax.ShapeDtypeStruct(shape, dtype)


def lane_ids(rows):
    return lax.broadcasted_iota(jnp.int32, (rows, LANES), 1)


def whole(shape):
    return pl.BlockSpec(shape, lambda *_: (0,) * len(shape))


def columns(rows16):
    pad = jnp.zeros((LANES - rows16.shape[0], LANES), f32)
    return jnp.transpose(jnp.concatenate([rows16, pad], axis=0))


def encode(value):
    largest = jnp.maximum(jnp.max(jnp.abs(value), axis=1, keepdims=True), 1e-30)
    codes = jnp.round(value * (32767.0 / largest)).astype(jnp.int32).astype(jnp.int16)
    return codes, largest * (1.0 / 32767.0)


def decode(codes, scale):
    return codes.astype(jnp.int32).astype(f32) * scale


def call(body, grid, n_prefetch, in_specs, out_specs, out_shape, scratch, args):
    return pl.pallas_call(
        body,
        grid_spec=pltpu.PrefetchScalarGridSpec(
            num_scalar_prefetch=n_prefetch,
            grid=grid,
            in_specs=in_specs,
            out_specs=out_specs,
            scratch_shapes=scratch,
        ),
        out_shape=out_shape,
        compiler_params=pltpu.CompilerParams(
            dimension_semantics=("arbitrary",) * len(grid), vmem_limit_bytes=56 << 20
        ),
    )(*args)


def place_scale(flags, even, odd, gain, splits, tok):
    half, n, feats = even.shape
    cols = 2 * half

    def body(flags_ref, even_ref, odd_ref, gain_ref, _, *outs):
        def put(src):
            wide = src[0].astype(f32)
            start = 0
            for i, tk in enumerate(splits):
                part = wide[start : start + tk]
                outs[2 * i][0] = (gain_ref[...] * part).astype(bf16)
                total = jnp.sum(part * part, axis=1, keepdims=True)
                outs[2 * i + 1][0] = jnp.broadcast_to(total, (tk, LANES))
                start += tk

        @pl.when(pl.program_id(0) < half)
        def _():
            put(even_ref)

        @pl.when(pl.program_id(0) >= half)
        def _():
            put(odd_ref)

    def slot(j, flags_ref):
        return (((j % half) * 2 + j // half) ^ flags_ref[1], 0, 0)

    out_specs, out_shape = [], []
    for tk in splits:
        out_specs += [pl.BlockSpec((1, tk, feats), slot), pl.BlockSpec((1, tk, LANES), slot)]
        out_shape += [sds((cols, tk, feats), bf16), sds((cols, tk, LANES), f32)]
    outs = call(
        body,
        (cols,),
        1,
        [
            pl.BlockSpec((1, n, feats), lambda j, _: (jnp.minimum(j, half - 1), 0, 0)),
            pl.BlockSpec((1, n, feats), lambda j, _: (jnp.maximum(j - half, 0), 0, 0)),
            whole((1, feats)),
            ANY,
        ],
        out_specs,
        out_shape,
        [],
        (flags, even, odd, gain, tok),
    )
    scaled = [o.reshape(cols * o.shape[1], feats) for o in outs[::2]]
    squares = [o.reshape(cols * o.shape[1], LANES) for o in outs[1::2]]
    return scaled, squares


def first_codes(scaled, squares, weight, tv, tok):
    count = len(scaled)
    tc, feats = scaled[0].shape
    vocab = weight.shape[1]
    tiles = vocab // tv
    nt = tiles // HALVES

    def body(*refs):
        xs = refs[:count]
        sqs = refs[count : 2 * count]
        w_ref = refs[2 * count]
        outs = refs[2 * count + 2 : 2 * count + 2 + 2 * HALVES * count]
        x_all, lanes_ref = refs[-2:]
        t = pl.program_id(0)

        @pl.when(t == 0)
        def _():
            for i in range(count):
                x_all[i * tc : (i + 1) * tc, :] = xs[i][...]

        product = jnp.dot(x_all[...], w_ref[...], preferred_element_type=f32)
        codes, scale = encode(product)
        lane = lane_ids(count * tc)
        for h in range(HALVES):

            @pl.when((t >= h * nt) & (t < (h + 1) * nt))
            def _():
                for i in range(count):
                    outs[(i * HALVES + h) * 2][...] = codes[i * tc : (i + 1) * tc]
                old = jnp.where(t == h * nt, 0.0, lanes_ref[...])
                lanes_ref[...] = jnp.where(lane == t - h * nt, scale, old)

            @pl.when(t == (h + 1) * nt - 1)
            def _():
                for i in range(count):
                    part = lanes_ref[i * tc : (i + 1) * tc, :]
                    part = jnp.where(lane_ids(tc) == SQ, sqs[i][...], part)
                    outs[(i * HALVES + h) * 2 + 1][...] = jnp.transpose(part)[:16]

    out_specs, out_shape = [], []
    for _ in range(count):
        for h in range(HALVES):
            out_specs += [
                pl.BlockSpec(
                    (tc, tv), lambda t, h=h: (0, jnp.clip(t - h * nt, 0, nt - 1))
                ),
                whole((16, LANES)),
            ]
            out_shape += [sds((tc, nt * tv), jnp.int16), sds((16, LANES), f32)]
    outs = call(
        body,
        (tiles,),
        0,
        [whole((tc, feats))] * count
        + [whole((tc, LANES))] * count
        + [pl.BlockSpec((feats, tv), lambda t: (0, t)), ANY],
        out_specs,
        out_shape,
        [pltpu.VMEM((count * tc, feats), bf16), pltpu.VMEM((count * tc, LANES), f32)],
        (*scaled, *squares, weight, tok),
    )
    return [(outs[2 * i], outs[2 * i + 1]) for i in range(count * HALVES)]


def add_codes(mine, got, tv, tok):
    tc, width = mine[0].shape
    nt = width // tv

    def body(a_ref, sa_ref, b_ref, sb_ref, _, o_ref, so_ref, ca, cb, lanes_ref):
        t = pl.program_id(0)

        @pl.when(t == 0)
        def _():
            ca[...] = columns(sa_ref[...])
            cb[...] = columns(sb_ref[...])

        lane = lane_ids(tc)
        here = lane == t
        scale_a = jnp.sum(jnp.where(here, ca[...], 0.0), axis=1, keepdims=True)
        scale_b = jnp.sum(jnp.where(here, cb[...], 0.0), axis=1, keepdims=True)
        codes, scale = encode(decode(a_ref[...], scale_a) + decode(b_ref[...], scale_b))
        o_ref[...] = codes
        old = jnp.where(t == 0, jnp.where(lane == SQ, ca[...] + cb[...], 0.0), lanes_ref[...])
        lanes_ref[...] = jnp.where(here, scale, old)

        @pl.when(t == nt - 1)
        def _():
            so_ref[...] = jnp.transpose(lanes_ref[...])[:16]

    tile = pl.BlockSpec((tc, tv), lambda t: (0, t))
    small = whole((16, LANES))
    return call(
        body,
        (nt,),
        0,
        [tile, small, tile, small, ANY],
        [tile, small],
        [sds((tc, width), jnp.int16), sds((16, LANES), f32)],
        [pltpu.VMEM((tc, LANES), f32)] * 3,
        (*mine, *got, tok),
    )


def code_specs(tc, tv, nt):
    specs = []
    for own in (1, 0):
        for h in range(HALVES):

            def index(t, flags, h=h, own=own):
                use = flags[0] if own else 1 - flags[0]
                return (0, jnp.clip(t - h * nt, 0, nt - 1) * use)

            specs.append(pl.BlockSpec((tc, tv), index))
    return specs + [whole((16, LANES))] * (2 * HALVES)


def load_columns(flags_ref, aux_refs, out_ref):
    for h in range(HALVES):
        own = columns(aux_refs[h][...])
        got = columns(aux_refs[HALVES + h][...])
        out_ref[h] = jnp.where(flags_ref[0] == 1, own, got)


def pick_tile(flags_ref, t, nt, refs, cols_ref, tile_ref):
    for h in range(HALVES):
        for own in (1, 0):

            @pl.when((t >= h * nt) & (t < (h + 1) * nt) & (flags_ref[0] == own))
            def _():
                here = lane_ids(LANES) == t - h * nt
                scale = jnp.sum(jnp.where(here, cols_ref[h], 0.0), axis=1, keepdims=True)
                tile_ref[...] = decode(refs[(1 - own) * HALVES + h][...], scale)


def local_stats(flags, pieces, target, all_feats, tv, tok):
    tc, width = pieces[0][0][0].shape
    nt = width // tv
    tiles = nt * HALVES

    def body(flags_ref, *refs):
        codes, aux = refs[: 2 * HALVES], refs[2 * HALVES : 4 * HALVES]
        tgt_ref, _, out_ref, cols_ref, tile_ref, run = refs[4 * HALVES :]
        t = pl.program_id(0)

        @pl.when(t == 0)
        def _():
            load_columns(flags_ref, aux, cols_ref)
            run[...] = jnp.where(lane_ids(tc) == 0, -jnp.inf, 0.0)

        pick_tile(flags_ref, t, nt, codes, cols_ref, tile_ref)
        inv = 1.0 / jnp.sqrt(cols_ref[0][:, SQ : SQ + 1] / all_feats + 1e-05)
        logits = tile_ref[...] * inv
        top, total, moment, found = (run[:, i : i + 1] for i in range(4))
        higher = jnp.maximum(top, jnp.max(logits, axis=1, keepdims=True))
        rescale = jnp.exp(top - higher)
        shifted = jnp.exp(logits - higher)
        total = total * rescale + jnp.sum(shifted, axis=1, keepdims=True)
        moment = moment * rescale + jnp.sum(shifted * logits, axis=1, keepdims=True)
        ids = lax.broadcasted_iota(jnp.int32, (tc, tv), 1) + (flags_ref[2] + t * tv)
        found = found + jnp.sum(
            jnp.where(ids == tgt_ref[...], logits, 0.0), axis=1, keepdims=True
        )
        lane = lane_ids(tc)
        packed = jnp.where(lane == 0, higher, jnp.where(lane == 1, total, 0.0))
        packed = jnp.where(lane == 2, moment, jnp.where(lane == 3, found, packed))
        run[...] = packed

        @pl.when(t == tiles - 1)
        def _():
            out_ref[...] = jnp.transpose(run[...])[:8]

    own = [p[0] for p in pieces]
    got = [p[1] for p in pieces]
    return call(
        body,
        (tiles,),
        1,
        code_specs(tc, tv, nt) + [whole((tc, 1)), ANY],
        whole((8, LANES)),
        sds((8, LANES), f32),
        [
            pltpu.VMEM((HALVES, tc, LANES), f32),
            pltpu.VMEM((tc, tv), f32),
            pltpu.VMEM((tc, LANES), f32),
        ],
        (
            flags,
            *[x[0] for x in own + got],
            *[x[1] for x in own + got],
            target,
            tok,
        ),
    )


def grad_and_feature(flags, pieces, target, stats, weight, cols, all_feats, tv, tok):
    tc, width = pieces[0][0][0].shape
    feats = weight.shape[0]
    nt = width // tv
    tiles = nt * HALVES
    tk = tc // cols

    def body(flags_ref, *refs):
        codes, aux = refs[: 2 * HALVES], refs[2 * HALVES : 4 * HALVES]
        tgt_ref, stats_ref, w_ref, _ = refs[4 * HALVES : 4 * HALVES + 4]
        g_ref, even_ref, odd_ref, info_ref = refs[4 * HALVES + 4 : 4 * HALVES + 8]
        cols_ref, stat_cols, tile_ref, acc = refs[4 * HALVES + 8 :]
        t = pl.program_id(0)

        @pl.when(t == 0)
        def _():
            load_columns(flags_ref, aux, cols_ref)
            stat_cols[...] = columns(stats_ref[...])
            acc[...] = jnp.zeros_like(acc)

        pick_tile(flags_ref, t, nt, codes, cols_ref, tile_ref)
        inv = 1.0 / jnp.sqrt(cols_ref[0][:, SQ : SQ + 1] / all_feats + 1e-05)
        logits = tile_ref[...] * inv
        top = stat_cols[:, 0:1]
        total = stat_cols[:, 1:2]
        probs = jnp.exp(logits - top) * (1.0 / total)
        ids = lax.broadcasted_iota(jnp.int32, (tc, tv), 1) + (flags_ref[2] + t * tv)
        grad = (inv * (probs - jnp.where(ids == tgt_ref[...], 1.0, 0.0))).astype(bf16)
        g_ref[...] = grad
        acc[...] += lax.dot_general(
            grad, w_ref[...], (((1,), (1,)), ((), ())), preferred_element_type=f32
        )

        @pl.when(t == tiles - 1)
        def _():
            for j in range(cols):
                start = pl.multiple_of((flags_ref[1] ^ j) * tk, tk)
                part = acc[pl.ds(start, tk), :].astype(bf16)
                if j % 2 == 0:
                    even_ref[j // 2] = part
                else:
                    odd_ref[j // 2] = part
            lane = lane_ids(tc)
            curvature = stat_cols[:, 2:3] / total - stat_cols[:, 3:4]
            factor = inv * inv * curvature
            info_ref[...] = jnp.transpose(jnp.where(lane == 0, factor, 0.0))[:8]

    own = [p[0] for p in pieces]
    got = [p[1] for p in pieces]
    slots = (cols // 2, tk, feats)
    return call(
        body,
        (tiles,),
        1,
        code_specs(tc, tv, nt)
        + [
            whole((tc, 1)),
            whole((8, LANES)),
            pl.BlockSpec((feats, tv), lambda t, _: (0, t)),
            ANY,
        ],
        [
            pl.BlockSpec((tc, tv), lambda t, _: (0, t)),
            whole(slots),
            whole(slots),
            whole((8, LANES)),
        ],
        [
            sds((tc, tiles * tv), bf16),
            sds(slots, bf16),
            sds(slots, bf16),
            sds((8, LANES), f32),
        ],
        [
            pltpu.VMEM((HALVES, tc, LANES), f32),
            pltpu.VMEM((tc, LANES), f32),
            pltpu.VMEM((tc, tv), f32),
            pltpu.VMEM((tc, feats), f32),
        ],
        (
            flags,
            *[x[0] for x in own + got],
            *[x[1] for x in own + got],
            target,
            stats,
            weight,
            tok,
        ),
    )


def head_product(scaled, grads, tv, tok):
    count = len(scaled)
    tc, feats = scaled[0].shape
    vocab = grads[0].shape[1]

    def body(*refs):
        xs, gs = refs[:count], refs[count : 2 * count]
        out_ref, flipped, g_all = refs[2 * count + 1 :]

        @pl.when(pl.program_id(0) == 0)
        def _():
            for i in range(count):
                flipped[:, i * tc : (i + 1) * tc] = jnp.transpose(xs[i][...])

        for i in range(count):
            g_all[i * tc : (i + 1) * tc, :] = gs[i][...]
        out_ref[...] = jnp.dot(flipped[...], g_all[...], preferred_element_type=f32).astype(bf16)

    return call(
        body,
        (vocab // tv,),
        0,
        [whole((tc, feats))] * count + [pl.BlockSpec((tc, tv), lambda t: (0, t))] * count + [ANY],
        pl.BlockSpec((feats, tv), lambda t: (0, t)),
        sds((feats, vocab), bf16),
        [pltpu.VMEM((feats, count * tc), bf16), pltpu.VMEM((count * tc, tv), bf16)],
        (*scaled, *grads, tok),
    )


def activate(flags, gate, up, cols, tok):
    tokens, width = gate.shape
    rows = tokens // cols
    half = cols // 2

    def body(flags_ref, gate_ref, up_ref, _, out_ref, small_ref):
        value = gate_ref[...].astype(f32)
        out_ref[...] = (value / (1.0 + jnp.exp(-value)) * up_ref[...].astype(f32)).astype(bf16)
        small_ref[...] = jnp.zeros_like(small_ref)

    source = pl.BlockSpec(
        (rows, width), lambda j, flags_ref: (((j % half) * 2 + j // half) ^ flags_ref[1], 0)
    )
    return call(
        body,
        (cols,),
        1,
        [source, source, ANY],
        [pl.BlockSpec((rows, width), lambda j, _: (j, 0)), whole((8, LANES))],
        [sds((tokens, width), bf16), sds((8, LANES), f32)],
        [],
        (flags, gate, up, tok),
    )


def partner(value, mask):
    size = lax.axis_size("col")
    return lax.ppermute(value, "col", [(i, i ^ mask) for i in range(size)])


def gather_slots(value):
    size = lax.axis_size("col")
    even = jnp.stack([value] + [partner(value, m) for m in range(2, size, 2)])
    return even, partner(even, 1)


def combine(left, right):
    biggest = jnp.maximum(left[0], right[0])
    left_scale = jnp.exp(left[0] - biggest)
    right_scale = jnp.exp(right[0] - biggest)
    return jnp.stack(
        [
            biggest,
            left[1] * left_scale + right[1] * right_scale,
            left[2] * left_scale + right[2] * right_scale,
            left[3] + right[3],
        ]
        + [left[4]] * 4
    )


def over_col(stats):
    step = 1
    while step < lax.axis_size("col"):
        stats = combine(stats, partner(stats, step))
        step *= 2
    return stats


def scatter_slots(even, odd):
    other = partner(odd, 1)
    summed = (even.astype(f32) + other.astype(f32)).astype(bf16)
    total = summed[0].astype(f32)
    for i in range(1, even.shape[0]):
        total = total + partner(summed[i], 2 * i).astype(f32)
    return total


def on_device(hidden_state, norm_gain, head_weight, targets, gate_act, up_act):
    tok_col, feats = hidden_state.shape
    vocab_part = head_weight.shape[1]
    cols = lax.axis_size("col")
    rows = lax.axis_size("row")
    half = rows // 2
    row = lax.axis_index("row")
    col = lax.axis_index("col")
    all_feats = feats * rows
    tk = tok_col // CHUNKS
    tc = tk * cols
    assert tc == LANES and rows % 2 == 0 and rows >= 4
    tv = min(1024, vocab_part // HALVES)
    inner = jnp.where((row == 0) | (row == rows - 1), 0, 1)
    flags = jnp.stack([inner, col, col * vocab_part]).astype(jnp.int32)
    gain = norm_gain[None, :]
    target_chunks = targets.reshape(cols, CHUNKS, tk)
    target_of = [target_chunks[:, k].reshape(tc, 1) for k in range(CHUNKS)]
    tok = norm_gain[:LANES].reshape(1, LANES)

    reduce_pairs = [[(s, s + 1), (rows - 1 - s, rows - 2 - s)] for s in range(half - 1)]
    reduce_pairs.append([(half - 1, half), (half, half - 1)])
    spread_pairs = [
        [(s + 1, s), (rows - 2 - s, rows - 1 - s)] for s in range(half - 2, -1, -1)
    ]

    def move(value, pairs):
        return tuple(lax.ppermute(x, "row", pairs) for x in value)

    even0, odd0 = gather_slots(hidden_state[:tk])
    even1, odd1 = gather_slots(hidden_state[tk:])
    scaled, squares = place_scale(flags, even0, odd0, gain, [tk], tok)
    tok = squares[0]
    current = first_codes(scaled, squares, head_weight, tv, tok)
    tok = current[-1][1]
    pending = {0: move(current[0], reduce_pairs[0])}
    more, more_squares = place_scale(flags, even1, odd1, gain, [tk] * (CHUNKS - 1), tok)
    scaled = scaled + more
    current = current + first_codes(more, more_squares, head_weight, tv, more_squares[0])
    tok = current[-1][1]
    activation, tok = activate(flags, gate_act, up_act, cols, tok)

    count = CHUNKS * HALVES
    final = {}
    stats = {}
    grads, hidden_grads = [], []

    def finish(k, tok):
        pieces = [final[k * HALVES + h] for h in range(HALVES)]
        grad, even, odd, info = grad_and_feature(
            flags, pieces, target_of[k], stats[k], head_weight, cols, all_feats, tv, tok
        )
        grads.append(grad)
        feature_grad = scatter_slots(even, odd)
        mine = lax.dynamic_slice_in_dim(info[0], col * tk, tk)
        wide = hidden_state[k * tk : (k + 1) * tk].astype(f32)
        hidden_grads.append((gain * feature_grad - wide * mine[:, None] / all_feats).astype(bf16))
        return info

    for i in range(count + 2 * half):
        for r in range(half):
            p = i - r
            if not 0 <= p < count:
                continue
            got = pending[p]
            if r == 0 and p + 1 < count:
                (codes, aux), got = lax.optimization_barrier((current[p + 1], got))
                pending[p + 1] = move((codes, aux), reduce_pairs[0])
            current[p] = add_codes(current[p], got, tv, tok)
            tok = current[p][1]
            pairs = reduce_pairs[r + 1] if r + 1 < half else spread_pairs[0]
            pending[p] = move(current[p], pairs)
        for q in range(half - 1):
            p = i - half - q
            if not 0 <= p < count:
                continue
            got = pending[p]
            if q + 1 < half - 1:
                s = half - 2 - q
                here = (row == s) | (row == rows - 1 - s)
                current[p] = tuple(jnp.where(here, g, c) for g, c in zip(got, current[p]))
                pending[p] = move(current[p], spread_pairs[q + 1])
            else:
                final[p] = (current[p], got)
                if p % HALVES == HALVES - 1:
                    k = p // HALVES
                    pieces = [final[k * HALVES + h] for h in range(HALVES)]
                    tok = local_stats(flags, pieces, target_of[k], all_feats, tv, tok)
                    stats[k] = over_col(tok)
                elif p // HALVES - 1 in stats:
                    tok = finish(p // HALVES - 1, tok)
    tok = finish(CHUNKS - 1, tok)

    head_grad = head_product(scaled, grads, min(512, vocab_part), tok)
    grad_hidden = jnp.concatenate(hidden_grads)
    even, odd = gather_slots(grad_hidden)
    down_sum = lax.dot_general(
        activation,
        jnp.concatenate([even, odd]).reshape(cols * tok_col, feats),
        (((0,), (0,)), ((), ())),
        preferred_element_type=f32,
    )
    return (head_grad, grad_hidden, down_sum.astype(bf16))


def solution(mesh):
    in_specs = (P("col", "row"), P("row"), P("row", "col"), P(), P(None, "col"), P(None, "col"))
    out_specs = (P("row", "col"), P("col", "row"), P("col", "row"))
    return jax.shard_map(
        on_device, mesh=mesh, in_specs=in_specs, out_specs=out_specs, check_vma=False
    )
```

```python
import jax
import jax.numpy as jnp
from jax import lax
from jax.experimental import pallas as pl
from jax.experimental.pallas import tpu as pltpu
from jax.sharding import PartitionSpec as P

PARTS = (2, 2, 2, 2)
GROUPS = ((0, 1), (2, 3))
DEPTH = 1
LANES = 128
TOP_CODE = 32700.0

f32 = jnp.float32
bf16 = jnp.bfloat16
i16 = jnp.int16
ANY = pl.BlockSpec(memory_space=pl.ANY)


def sds(shape, dtype):
    return jax.ShapeDtypeStruct(shape, dtype)


def lane_ids(rows):
    return lax.broadcasted_iota(jnp.int32, (rows, LANES), 1)


def whole(shape):
    return pl.BlockSpec(shape, lambda *_: (0,) * len(shape))


def columns(rows8):
    pad = jnp.zeros((LANES - rows8.shape[0], LANES), f32)
    return jnp.transpose(jnp.concatenate([rows8, pad], axis=0))


def to_rows(*cols):
    lane = lane_ids(LANES)
    packed = jnp.zeros((LANES, LANES), f32)
    for i, col in enumerate(cols):
        packed = jnp.where(lane == i, col, packed)
    return jnp.transpose(packed)[:8]


def call(body, grid, n_prefetch, in_specs, out_specs, out_shape, scratch, args):
    return pl.pallas_call(
        body,
        grid_spec=pltpu.PrefetchScalarGridSpec(
            num_scalar_prefetch=n_prefetch,
            grid=grid,
            in_specs=in_specs,
            out_specs=out_specs,
            scratch_shapes=scratch,
        ),
        out_shape=out_shape,
        compiler_params=pltpu.CompilerParams(
            dimension_semantics=("arbitrary",) * len(grid), vmem_limit_bytes=56 << 20
        ),
    )(*args)


def logit_parts(flags, even, odd, gain, weight, count, tv, tok):
    half, n, feats = even.shape
    cols = 2 * half
    tk = n // count
    tc = tk * cols
    vocab = weight.shape[1]
    tiles = vocab // tv

    def body(flags_ref, even_ref, odd_ref, gain_ref, w_ref, _, *refs):
        outs, (x_all, squares, largest) = refs[: 3 * count], refs[3 * count :]
        t = pl.program_id(0)

        @pl.when(t == 0)
        def _():
            for j in range(cols):
                wide = (odd_ref if j % 2 else even_ref)[j // 2].astype(f32)
                value = (gain_ref[...] * wide).astype(bf16)
                total = jnp.broadcast_to(jnp.sum(wide * wide, axis=1, keepdims=True), (n, LANES))
                for i in range(count):
                    start = pl.multiple_of((flags_ref[1] ^ j) * tk, tk)
                    part = slice(i * tk, (i + 1) * tk)
                    outs[3 * i][pl.ds(start, tk), :] = value[part]
                    squares[i, pl.ds(start, tk), :] = total[part]
            for i in range(count):
                x_all[i * tc : (i + 1) * tc, :] = outs[3 * i][...]
            largest[...] = jnp.zeros_like(largest)

        product = jnp.dot(x_all[...], w_ref[...], preferred_element_type=f32)
        for i in range(count):
            outs[3 * i + 1][...] = product[i * tc : (i + 1) * tc]
        size = jnp.abs(product)
        best = largest[...]
        for s in range(0, tv, LANES):
            best = jnp.maximum(best, size[:, s : s + LANES])
        largest[...] = best

        @pl.when(t == tiles - 1)
        def _():
            for i in range(count):
                top = jnp.max(largest[i * tc : (i + 1) * tc, :], axis=1, keepdims=True)
                outs[3 * i + 2][...] = to_rows(top, squares[i][:, 0:1])

    out_specs, out_shape = [], []
    for _ in range(count):
        out_specs += [
            whole((tc, feats)),
            pl.BlockSpec((tc, tv), lambda t, _: (0, t)),
            whole((8, LANES)),
        ]
        out_shape += [sds((tc, feats), bf16), sds((tc, vocab), f32), sds((8, LANES), f32)]
    outs = call(
        body,
        (tiles,),
        1,
        [
            whole((half, n, feats)),
            whole((half, n, feats)),
            whole((1, feats)),
            pl.BlockSpec((feats, tv), lambda t, _: (0, t)),
            ANY,
        ],
        out_specs,
        out_shape,
        [
            pltpu.VMEM((count * tc, feats), bf16),
            pltpu.VMEM((count, tc, LANES), f32),
            pltpu.VMEM((count * tc, LANES), f32),
        ],
        (flags, even, odd, gain, weight, tok),
    )
    return outs[::3], outs[1::3], outs[2::3]


def to_codes(product, rows8, parts, tok):
    tc, vocab = product.shape
    width = vocab // parts
    tv = min(width, 2048)
    nt = width // tv

    def body(p_ref, rows_ref, _, *refs):
        outs, factor = refs[:-1], refs[-1]
        t = pl.program_id(0)

        @pl.when(t == 0)
        def _():
            factor[...] = columns(TOP_CODE / jnp.maximum(rows_ref[...], 1e-30))

        codes = jnp.round(p_ref[...] * factor[:, 0:1]).astype(jnp.int32).astype(i16)
        for h in range(parts):

            @pl.when((t >= h * nt) & (t < (h + 1) * nt))
            def _():
                outs[h][...] = codes

    return call(
        body,
        (parts * nt,),
        0,
        [pl.BlockSpec((tc, tv), lambda t: (0, t)), whole((8, LANES)), ANY],
        [
            pl.BlockSpec((tc, tv), lambda t, h=h: (0, jnp.clip(t - h * nt, 0, nt - 1)))
            for h in range(parts)
        ],
        [sds((tc, width), i16)] * parts,
        [pltpu.VMEM((tc, LANES), f32)],
        (product, rows8, tok),
    )


def local_stats(flags, own, got, rows8, target, all_feats, tok):
    parts = len(own)
    tc, width = own[0].shape
    tb = 32
    tv = min(width, 1024)

    def body(flags_ref, *refs):
        own_refs, got_refs = refs[:parts], refs[parts : 2 * parts]
        rows_ref, tgt_ref, _, out_ref, cols_ref, codes, result = refs[2 * parts :]
        i = pl.program_id(0)

        @pl.when(i == 0)
        def _():
            cols_ref[...] = columns(rows_ref[...])

        for h in range(parts):
            for use, source in ((1, own_refs[h]), (0, got_refs[h])):

                @pl.when(flags_ref[0] == use)
                def _():
                    codes[:, h * width : (h + 1) * width] = source[...]

        cols = cols_ref[pl.ds(pl.multiple_of(i * tb, tb), tb), :]
        inv = 1.0 / jnp.sqrt(cols[:, 1:2] / all_feats + 1e-05)
        factor = jnp.maximum(cols[:, 0:1], 1e-30) * (inv * (1.0 / TOP_CODE))

        best = jnp.full((tb, LANES), -40000.0, f32)
        for s in range(0, parts * width, tv):
            tile = codes[:, s : s + tv].astype(jnp.int32).astype(f32)
            for u in range(0, tv, LANES):
                best = jnp.maximum(best, tile[:, u : u + LANES])
        top = jnp.max(best, axis=1, keepdims=True) * factor
        total = jnp.zeros((tb, LANES), f32)
        moment = jnp.zeros((tb, LANES), f32)
        found = jnp.zeros((tb, LANES), f32)
        wanted = tgt_ref[...] - flags_ref[2]
        lane = lane_ids(tb)
        for s in range(0, parts * width, LANES):
            logits = codes[:, s : s + LANES].astype(jnp.int32).astype(f32) * factor
            shifted = jnp.exp(logits - top)
            total = total + shifted
            moment = moment + shifted * logits
            found = found + jnp.where(lane == wanted - s, logits, 0.0)
        values = [top] + [jnp.sum(v, axis=1, keepdims=True) for v in (total, moment, found)]
        packed = jnp.zeros((tb, LANES), f32)
        for n, value in enumerate(values):
            packed = jnp.where(lane == n, value, packed)
        result[pl.ds(pl.multiple_of(i * tb, tb), tb), :] = packed

        @pl.when(i == tc // tb - 1)
        def _():
            out_ref[...] = jnp.transpose(result[...])[:8]

    specs = [pl.BlockSpec((tb, width), lambda i, flags: (i * flags[0], 0))] * parts
    specs += [pl.BlockSpec((tb, width), lambda i, flags: (i * (1 - flags[0]), 0))] * parts
    return call(
        body,
        (tc // tb,),
        1,
        specs + [whole((8, LANES)), pl.BlockSpec((tb, 1), lambda i, _: (i, 0)), ANY],
        whole((8, LANES)),
        sds((8, LANES), f32),
        [
            pltpu.VMEM((tc, LANES), f32),
            pltpu.VMEM((tb, parts * width), i16),
            pltpu.VMEM((tc, LANES), f32),
        ],
        (flags, *own, *got, rows8, target, tok),
    )


def grad_and_feature(flags, pieces, rows8, target, stats, weight, cols, all_feats, tv, tok):
    count = len(pieces)
    feats, vocab = weight.shape
    tc = LANES
    tk = tc // cols
    tiles = vocab // tv
    refs_of = [2 * len(own) for own, _ in pieces]
    total_refs = sum(refs_of)

    def body(flags_ref, *refs):
        codes = refs[:total_refs]
        rows_refs = refs[total_refs : total_refs + count]
        tgt_refs = refs[total_refs + count : total_refs + 2 * count]
        stats_ref, w_ref, _ = refs[total_refs + 2 * count : total_refs + 2 * count + 3]
        rest = refs[total_refs + 2 * count + 3 :]
        g_refs, (even_ref, odd_ref, info_ref) = rest[:count], rest[count : count + 3]
        cols_ref, stat_cols, tile_ref, g_all, acc, flipped = rest[count + 3 :]
        t = pl.program_id(0)

        @pl.when(t == 0)
        def _():
            for i in range(count):
                stat = columns(stats_ref[i])
                rows = columns(rows_refs[i][...])
                inv = 1.0 / jnp.sqrt(rows[:, 1:2] / all_feats + 1e-05)
                factor = jnp.maximum(rows[:, 0:1], 1e-30) * (inv * (1.0 / TOP_CODE))
                over = inv / stat[:, 1:2]
                curve = inv * inv * (stat[:, 2:3] / stat[:, 1:2] - stat[:, 3:4])
                lane = lane_ids(tc)
                packed = jnp.where(lane == 0, factor, jnp.where(lane == 1, over, 0.0))
                packed = jnp.where(lane == 2, inv, jnp.where(lane == 3, curve, packed))
                cols_ref[i] = packed
                stat_cols[i] = stat
            acc[...] = jnp.zeros_like(acc)

        base = 0
        for i, (own, _) in enumerate(pieces):
            parts = len(own)
            nt = tiles // parts
            for h in range(parts):
                for use, place in ((1, base + h), (0, base + parts + h)):

                    @pl.when((t >= h * nt) & (t < (h + 1) * nt) & (flags_ref[0] == use))
                    def _():
                        tile_ref[i] = codes[place][...]

            base += 2 * parts
            column = lambda n: cols_ref[i][:, n : n + 1]
            wanted = tgt_refs[i][...] - (flags_ref[2] + t * tv)
            factor, over, inv, top = column(0), column(1), column(2), stat_cols[i][:, 0:1]
            lane = lane_ids(tc)
            for s in range(0, tv, LANES):
                logits = tile_ref[i][:, s : s + LANES].astype(jnp.int32).astype(f32) * factor
                probs = jnp.exp(logits - top) * over
                grad = (probs - jnp.where(lane == wanted - s, inv, 0.0)).astype(bf16)
                g_refs[i][:, s : s + LANES] = grad
                g_all[i * tc : (i + 1) * tc, s : s + LANES] = grad
        acc[...] += lax.dot_general(
            w_ref[...], g_all[...], (((1,), (1,)), ((), ())), preferred_element_type=f32
        )

        @pl.when(t == tiles - 1)
        def _():
            for i in range(count):
                flipped[...] = jnp.transpose(acc[:, i * tc : (i + 1) * tc])
                for j in range(cols):
                    start = pl.multiple_of((flags_ref[1] ^ j) * tk, tk)
                    part = flipped[pl.ds(start, tk), :].astype(bf16)
                    out_ref = odd_ref if j % 2 else even_ref
                    out_ref[j // 2, i * tk : (i + 1) * tk, :] = part
                info_ref[i] = to_rows(cols_ref[i][:, 3:4])

    code_specs, code_args = [], []
    for own, got in pieces:
        nt = tiles // len(own)
        for use, arrays in ((1, own), (0, got)):
            for h, array in enumerate(arrays):

                def index(t, flags, h=h, use=use, nt=nt):
                    on = flags[0] if use else 1 - flags[0]
                    return (0, jnp.clip(t - h * nt, 0, nt - 1) * on)

                code_specs.append(pl.BlockSpec((tc, tv), index))
                code_args.append(array)
    slots = (cols // 2, count * tk, feats)
    outs = call(
        body,
        (tiles,),
        1,
        code_specs
        + [whole((8, LANES))] * count
        + [whole((tc, 1))] * count
        + [whole((count, 8, LANES)), pl.BlockSpec((feats, tv), lambda t, _: (0, t)), ANY],
        [pl.BlockSpec((tc, tv), lambda t, _: (0, t))] * count
        + [whole(slots), whole(slots), whole((count, 8, LANES))],
        [sds((tc, vocab), bf16)] * count
        + [sds(slots, bf16), sds(slots, bf16), sds((count, 8, LANES), f32)],
        [
            pltpu.VMEM((count, tc, LANES), f32),
            pltpu.VMEM((count, tc, LANES), f32),
            pltpu.VMEM((count, tc, tv), i16),
            pltpu.VMEM((count * tc, tv), bf16),
            pltpu.VMEM((feats, count * tc), f32),
            pltpu.VMEM((tc, feats), f32),
        ],
        (flags, *code_args, *rows8, *target, stats, weight, tok),
    )
    return outs[:count], outs[count], outs[count + 1], outs[count + 2]


def head_product(scaled, grads, tv, tok):
    count = len(scaled)
    tc, feats = scaled[0].shape
    vocab = grads[0].shape[1]

    def body(*refs):
        xs, gs = refs[:count], refs[count : 2 * count]
        out_ref, flipped, g_all = refs[2 * count + 1 :]

        @pl.when(pl.program_id(0) == 0)
        def _():
            for i in range(count):
                flipped[:, i * tc : (i + 1) * tc] = jnp.transpose(xs[i][...])

        for i in range(count):
            g_all[i * tc : (i + 1) * tc, :] = gs[i][...]
        out_ref[...] = jnp.dot(flipped[...], g_all[...], preferred_element_type=f32).astype(bf16)

    return call(
        body,
        (vocab // tv,),
        0,
        [whole((tc, feats))] * count + [pl.BlockSpec((tc, tv), lambda t: (0, t))] * count + [ANY],
        pl.BlockSpec((feats, tv), lambda t: (0, t)),
        sds((feats, vocab), bf16),
        [pltpu.VMEM((feats, count * tc), bf16), pltpu.VMEM((count * tc, tv), bf16)],
        (*scaled, *grads, tok),
    )


def activate(flags, gate, up, cols, tok):
    tokens, width = gate.shape
    rows = tokens // cols
    half = cols // 2

    def body(flags_ref, gate_ref, up_ref, _, out_ref, small_ref):
        value = gate_ref[...].astype(f32)
        out_ref[...] = (value / (1.0 + jnp.exp(-value)) * up_ref[...].astype(f32)).astype(bf16)
        small_ref[...] = jnp.zeros_like(small_ref)

    source = pl.BlockSpec(
        (rows, width), lambda j, flags_ref: (((j % half) * 2 + j // half) ^ flags_ref[1], 0)
    )
    return call(
        body,
        (cols,),
        1,
        [source, source, ANY],
        [pl.BlockSpec((rows, width), lambda j, _: (j, 0)), whole((8, LANES))],
        [sds((tokens, width), bf16), sds((8, LANES), f32)],
        [],
        (flags, gate, up, tok),
    )


def partner(value, mask, axis="col"):
    size = lax.axis_size(axis)
    return lax.ppermute(value, axis, [(i, i ^ mask) for i in range(size)])


def gather_slots(value):
    size = lax.axis_size("col")
    even = jnp.stack([value] + [partner(value, m) for m in range(2, size, 2)])
    return even, partner(even, 1)


def combine(left, right):
    biggest = jnp.maximum(left[:, 0], right[:, 0])
    left_scale = jnp.exp(left[:, 0] - biggest)
    right_scale = jnp.exp(right[:, 0] - biggest)
    return jnp.stack(
        [
            biggest,
            left[:, 1] * left_scale + right[:, 1] * right_scale,
            left[:, 2] * left_scale + right[:, 2] * right_scale,
            left[:, 3] + right[:, 3],
        ]
        + [left[:, 4]] * 4,
        axis=1,
    )


def over_col(stats):
    step = 1
    while step < lax.axis_size("col"):
        stats = combine(stats, partner(stats, step))
        step *= 2
    return stats


def over_row(value):
    step = 1
    while step < lax.axis_size("row"):
        value = value + partner(value, step, "row")
        step *= 2
    return value


def scatter_slots(even, odd):
    other = partner(odd, 1)
    summed = (even.astype(f32) + other.astype(f32)).astype(bf16)
    total = summed[0].astype(f32)
    for i in range(1, even.shape[0]):
        total = total + partner(summed[i], 2 * i).astype(f32)
    return total


def on_device(hidden_state, norm_gain, head_weight, targets, gate_act, up_act):
    tok_col, feats = hidden_state.shape
    vocab_part = head_weight.shape[1]
    cols = lax.axis_size("col")
    rows = lax.axis_size("row")
    half = rows // 2
    row = lax.axis_index("row")
    col = lax.axis_index("col")
    all_feats = feats * rows
    chunks = len(PARTS)
    tk = tok_col // chunks
    tc = tk * cols
    assert tc == LANES and rows in (4, 8, 16) and cols & (cols - 1) == 0
    tv = vocab_part // max(8, *PARTS)
    inner = jnp.where((row == 0) | (row == rows - 1), 0, 1)
    flags = jnp.stack([inner, col, col * vocab_part]).astype(jnp.int32)
    gain = norm_gain[None, :]
    target_chunks = targets.reshape(cols, chunks, tk)
    target_of = [target_chunks[:, k].reshape(tc, 1) for k in range(chunks)]
    tok = norm_gain[:LANES].reshape(1, LANES)

    reduce_pairs = [[(s, s + 1), (rows - 1 - s, rows - 2 - s)] for s in range(half - 1)]
    reduce_pairs.append([(half - 1, half), (half, half - 1)])
    spread_pairs = [
        [(s + 1, s), (rows - 2 - s, rows - 1 - s)] for s in range(half - 2, -1, -1)
    ]

    def move(value, pairs):
        return lax.ppermute(value, "row", pairs)

    even0, odd0 = gather_slots(hidden_state[:tk])
    even1, odd1 = gather_slots(hidden_state[tk:])
    scaled, products, rows8 = logit_parts(flags, even0, odd0, gain, head_weight, 1, tv, tok)
    rows8 = [over_row(rows8[0])]
    current = list(to_codes(products[0], rows8[0], PARTS[0], tok))
    pending = {0: move(current[0], reduce_pairs[0])}
    more, products, more_rows = logit_parts(
        flags, even1, odd1, gain, head_weight, chunks - 1, tv, current[0]
    )
    scaled = list(scaled) + list(more)
    more_rows = over_row(jnp.stack(more_rows))
    activation, tok = activate(flags, gate_act, up_act, cols, more[0])
    for k in range(1, chunks):
        rows8.append(more_rows[k - 1])
        made = to_codes(products[k - 1], rows8[k], PARTS[k], tok)
        tok = made[0]
        current += list(made)

    chunk_of = [k for k in range(chunks) for _ in range(PARTS[k])]
    count = len(chunk_of)
    first_of = [chunk_of.index(k) for k in range(chunks)]
    arrived = {}
    final = {}
    stats = {}
    grads, hidden_grads, gathered = [], [], []

    def own_and_got(k):
        span = range(first_of[k], first_of[k] + PARTS[k])
        return [final[p][0] for p in span], [final[p][1] for p in span]

    def finish(group, tok):
        together = over_col(jnp.stack([stats[k] for k in group]))
        grad, even, odd, info = grad_and_feature(
            flags,
            [own_and_got(k) for k in group],
            [rows8[k] for k in group],
            [target_of[k] for k in group],
            together,
            head_weight,
            cols,
            all_feats,
            tv,
            tok,
        )
        grads.extend(grad)
        feature_grad = scatter_slots(even, odd)
        mine = lax.dynamic_slice_in_dim(info[:, 0], col * tk, tk, axis=1).reshape(-1)
        span = slice(group[0] * tk, (group[-1] + 1) * tk)
        wide = hidden_state[span].astype(f32)
        result = (gain * feature_grad - wide * mine[:, None] / all_feats).astype(bf16)
        hidden_grads.append(result)
        gathered.append(gather_slots(result))
        return info

    def add(left, right, tok):
        left, right, _ = lax.optimization_barrier((left, right, tok))
        return left + right

    for i in range(count + 2 * half - 1):
        for r in range(half):
            p = i - r
            if not 0 <= p < count:
                continue
            got = pending[p]
            if r == 0:
                for n in range(p + 1, min(p + 1 + DEPTH, count)):
                    if n not in pending and n - DEPTH <= p:
                        codes, got = lax.optimization_barrier((current[n], got))
                        pending[n] = move(codes, reduce_pairs[0])
            tok = current[p] = add(current[p], got, tok)
            pairs = reduce_pairs[r + 1] if r + 1 < half else spread_pairs[0]
            pending[p] = move(current[p], pairs)
        for q in range(half - 1):
            p = i - half - q
            if not 0 <= p < count:
                continue
            got = pending[p]
            if q + 1 < half - 1:
                s = half - 2 - q
                here = (row == s) | (row == rows - 1 - s)
                current[p] = jnp.where(here, got, current[p])
                pending[p] = move(current[p], spread_pairs[q + 1])
                continue
            final[p] = (current[p], got)
            k = chunk_of[p]
            if p + 1 == count or chunk_of[p + 1] != k:
                own, got = own_and_got(k)
                tok = stats[k] = local_stats(
                    flags, own, got, rows8[k], target_of[k], all_feats, tok
                )
            elif len(grads) == 0 and GROUPS[0][-1] in stats:
                tok = finish(GROUPS[0], tok)
    for group in GROUPS[1 if grads else 0 :]:
        tok = finish(group, tok)

    head_grad = head_product(scaled, grads, min(512, vocab_part), tok)
    grad_hidden = jnp.concatenate(hidden_grads)
    gathered = jnp.concatenate([jnp.concatenate(pair) for pair in gathered], axis=1)
    down_sum = lax.dot_general(
        activation,
        gathered.reshape(cols * tok_col, feats),
        (((0,), (0,)), ((), ())),
        preferred_element_type=f32,
    )
    return (head_grad, grad_hidden, down_sum.astype(bf16))


def solution(mesh):
    in_specs = (P("col", "row"), P("row"), P("row", "col"), P(), P(None, "col"), P(None, "col"))
    out_specs = (P("row", "col"), P("col", "row"), P("col", "row"))
    return jax.shard_map(
        on_device, mesh=mesh, in_specs=in_specs, out_specs=out_specs, check_vma=False
    )
```

```python
import jax
import jax.numpy as jnp
from jax import lax
from jax.experimental import pallas as pl
from jax.experimental.pallas import tpu as pltpu
from jax.sharding import PartitionSpec as P

PARTS = (4, 2, 2, 4)
GROUPS = ((0, 1), (2,), (3,))
DEPTH = 2
HEAD_PARTS = 4
LANES = 128
TOP_CODE = 32700.0

f32 = jnp.float32
bf16 = jnp.bfloat16
i16 = jnp.int16
ANY = pl.BlockSpec(memory_space=pl.ANY)


def sds(shape, dtype):
    return jax.ShapeDtypeStruct(shape, dtype)


def lane_ids(rows):
    return lax.broadcasted_iota(jnp.int32, (rows, LANES), 1)


def whole(shape):
    return pl.BlockSpec(shape, lambda *_: (0,) * len(shape))


def columns(rows8):
    pad = jnp.zeros((LANES - rows8.shape[0], LANES), f32)
    return jnp.transpose(jnp.concatenate([rows8, pad], axis=0))


def to_rows(*cols):
    lane = lane_ids(LANES)
    packed = jnp.zeros((LANES, LANES), f32)
    for i, col in enumerate(cols):
        packed = jnp.where(lane == i, col, packed)
    return jnp.transpose(packed)[:8]


def call(body, grid, n_prefetch, in_specs, out_specs, out_shape, scratch, args):
    return pl.pallas_call(
        body,
        grid_spec=pltpu.PrefetchScalarGridSpec(
            num_scalar_prefetch=n_prefetch,
            grid=grid,
            in_specs=in_specs,
            out_specs=out_specs,
            scratch_shapes=scratch,
        ),
        out_shape=out_shape,
        compiler_params=pltpu.CompilerParams(
            dimension_semantics=("arbitrary",) * len(grid), vmem_limit_bytes=56 << 20
        ),
    )(*args)


def logit_parts(flags, even, odd, gain, weight, count, tv, tok):
    half, n, feats = even.shape
    cols = 2 * half
    tk = n // count
    tc = tk * cols
    vocab = weight.shape[1]
    tiles = vocab // tv

    def body(flags_ref, even_ref, odd_ref, gain_ref, w_ref, _, *refs):
        outs, (x_all, squares, largest) = refs[: 3 * count], refs[3 * count :]
        t = pl.program_id(0)

        @pl.when(t == 0)
        def _():
            for j in range(cols):
                wide = (odd_ref if j % 2 else even_ref)[j // 2].astype(f32)
                value = (gain_ref[...] * wide).astype(bf16)
                total = jnp.broadcast_to(jnp.sum(wide * wide, axis=1, keepdims=True), (n, LANES))
                for i in range(count):
                    start = pl.multiple_of((flags_ref[1] ^ j) * tk, tk)
                    part = slice(i * tk, (i + 1) * tk)
                    outs[3 * i][pl.ds(start, tk), :] = value[part]
                    squares[i, pl.ds(start, tk), :] = total[part]
            for i in range(count):
                x_all[i * tc : (i + 1) * tc, :] = outs[3 * i][...]
            largest[...] = jnp.zeros_like(largest)

        product = jnp.dot(x_all[...], w_ref[...], preferred_element_type=f32)
        for i in range(count):
            outs[3 * i + 1][...] = product[i * tc : (i + 1) * tc]
        size = jnp.abs(product)
        best = largest[...]
        for s in range(0, tv, LANES):
            best = jnp.maximum(best, size[:, s : s + LANES])
        largest[...] = best

        @pl.when(t == tiles - 1)
        def _():
            for i in range(count):
                top = jnp.max(largest[i * tc : (i + 1) * tc, :], axis=1, keepdims=True)
                outs[3 * i + 2][...] = to_rows(top, squares[i][:, 0:1])

    out_specs, out_shape = [], []
    for _ in range(count):
        out_specs += [
            whole((tc, feats)),
            pl.BlockSpec((tc, tv), lambda t, _: (0, t)),
            whole((8, LANES)),
        ]
        out_shape += [sds((tc, feats), bf16), sds((tc, vocab), f32), sds((8, LANES), f32)]
    outs = call(
        body,
        (tiles,),
        1,
        [
            whole((half, n, feats)),
            whole((half, n, feats)),
            whole((1, feats)),
            pl.BlockSpec((feats, tv), lambda t, _: (0, t)),
            ANY,
        ],
        out_specs,
        out_shape,
        [
            pltpu.VMEM((count * tc, feats), bf16),
            pltpu.VMEM((count, tc, LANES), f32),
            pltpu.VMEM((count * tc, LANES), f32),
        ],
        (flags, even, odd, gain, weight, tok),
    )
    return outs[::3], outs[1::3], outs[2::3]


def to_codes(product, rows8, parts, tok):
    tc, vocab = product.shape
    width = vocab // parts
    tv = min(width, 2048)
    nt = width // tv

    def body(p_ref, rows_ref, _, *refs):
        outs, factor = refs[:-1], refs[-1]
        t = pl.program_id(0)

        @pl.when(t == 0)
        def _():
            factor[...] = columns(TOP_CODE / jnp.maximum(rows_ref[...], 1e-30))

        codes = jnp.round(p_ref[...] * factor[:, 0:1]).astype(jnp.int32).astype(i16)
        for h in range(parts):

            @pl.when((t >= h * nt) & (t < (h + 1) * nt))
            def _():
                outs[h][...] = codes

    return call(
        body,
        (parts * nt,),
        0,
        [pl.BlockSpec((tc, tv), lambda t: (0, t)), whole((8, LANES)), ANY],
        [
            pl.BlockSpec((tc, tv), lambda t, h=h: (0, jnp.clip(t - h * nt, 0, nt - 1)))
            for h in range(parts)
        ],
        [sds((tc, width), i16)] * parts,
        [pltpu.VMEM((tc, LANES), f32)],
        (product, rows8, tok),
    )


def local_stats(flags, own, got, rows8, target, all_feats, tok):
    parts = len(own)
    tc, width = own[0].shape
    tb = 32
    tv = min(width, 1024)

    def body(flags_ref, *refs):
        own_refs, got_refs = refs[:parts], refs[parts : 2 * parts]
        rows_ref, tgt_ref, _, out_ref, cols_ref, codes, result = refs[2 * parts :]
        i = pl.program_id(0)

        @pl.when(i == 0)
        def _():
            cols_ref[...] = columns(rows_ref[...])

        for h in range(parts):
            for use, source in ((1, own_refs[h]), (0, got_refs[h])):

                @pl.when(flags_ref[0] == use)
                def _():
                    codes[:, h * width : (h + 1) * width] = source[...]

        cols = cols_ref[pl.ds(pl.multiple_of(i * tb, tb), tb), :]
        inv = 1.0 / jnp.sqrt(cols[:, 1:2] / all_feats + 1e-05)
        factor = jnp.maximum(cols[:, 0:1], 1e-30) * (inv * (1.0 / TOP_CODE))

        best = jnp.full((tb, LANES), -40000.0, f32)
        for s in range(0, parts * width, tv):
            tile = codes[:, s : s + tv].astype(jnp.int32).astype(f32)
            for u in range(0, tv, LANES):
                best = jnp.maximum(best, tile[:, u : u + LANES])
        top = jnp.max(best, axis=1, keepdims=True) * factor
        total = jnp.zeros((tb, LANES), f32)
        moment = jnp.zeros((tb, LANES), f32)
        found = jnp.zeros((tb, LANES), f32)
        wanted = tgt_ref[...] - flags_ref[2]
        lane = lane_ids(tb)
        for s in range(0, parts * width, LANES):
            logits = codes[:, s : s + LANES].astype(jnp.int32).astype(f32) * factor
            shifted = jnp.exp(logits - top)
            total = total + shifted
            moment = moment + shifted * logits
            found = found + jnp.where(lane == wanted - s, logits, 0.0)
        values = [top] + [jnp.sum(v, axis=1, keepdims=True) for v in (total, moment, found)]
        packed = jnp.zeros((tb, LANES), f32)
        for n, value in enumerate(values):
            packed = jnp.where(lane == n, value, packed)
        result[pl.ds(pl.multiple_of(i * tb, tb), tb), :] = packed

        @pl.when(i == tc // tb - 1)
        def _():
            out_ref[...] = jnp.transpose(result[...])[:8]

    specs = [pl.BlockSpec((tb, width), lambda i, flags: (i * flags[0], 0))] * parts
    specs += [pl.BlockSpec((tb, width), lambda i, flags: (i * (1 - flags[0]), 0))] * parts
    return call(
        body,
        (tc // tb,),
        1,
        specs + [whole((8, LANES)), pl.BlockSpec((tb, 1), lambda i, _: (i, 0)), ANY],
        whole((8, LANES)),
        sds((8, LANES), f32),
        [
            pltpu.VMEM((tc, LANES), f32),
            pltpu.VMEM((tb, parts * width), i16),
            pltpu.VMEM((tc, LANES), f32),
        ],
        (flags, *own, *got, rows8, target, tok),
    )


def grad_and_feature(flags, pieces, rows8, target, stats, weight, cols, all_feats, tv, tok):
    count = len(pieces)
    feats, vocab = weight.shape
    tc = LANES
    tk = tc // cols
    tiles = vocab // tv
    refs_of = [2 * len(own) for own, _ in pieces]
    total_refs = sum(refs_of)

    def body(flags_ref, *refs):
        codes = refs[:total_refs]
        rows_refs = refs[total_refs : total_refs + count]
        tgt_refs = refs[total_refs + count : total_refs + 2 * count]
        stats_ref, w_ref, _ = refs[total_refs + 2 * count : total_refs + 2 * count + 3]
        rest = refs[total_refs + 2 * count + 3 :]
        g_refs, (even_ref, odd_ref, info_ref) = rest[:count], rest[count : count + 3]
        cols_ref, stat_cols, tile_ref, g_all, acc, flipped = rest[count + 3 :]
        t = pl.program_id(0)

        @pl.when(t == 0)
        def _():
            for i in range(count):
                stat = columns(stats_ref[i])
                rows = columns(rows_refs[i][...])
                inv = 1.0 / jnp.sqrt(rows[:, 1:2] / all_feats + 1e-05)
                factor = jnp.maximum(rows[:, 0:1], 1e-30) * (inv * (1.0 / TOP_CODE))
                over = inv / stat[:, 1:2]
                curve = inv * inv * (stat[:, 2:3] / stat[:, 1:2] - stat[:, 3:4])
                lane = lane_ids(tc)
                packed = jnp.where(lane == 0, factor, jnp.where(lane == 1, over, 0.0))
                packed = jnp.where(lane == 2, inv, jnp.where(lane == 3, curve, packed))
                cols_ref[i] = packed
                stat_cols[i] = stat
            acc[...] = jnp.zeros_like(acc)

        base = 0
        for i, (own, _) in enumerate(pieces):
            parts = len(own)
            nt = tiles // parts
            for h in range(parts):
                for use, place in ((1, base + h), (0, base + parts + h)):

                    @pl.when((t >= h * nt) & (t < (h + 1) * nt) & (flags_ref[0] == use))
                    def _():
                        tile_ref[i] = codes[place][...]

            base += 2 * parts
            column = lambda n: cols_ref[i][:, n : n + 1]
            wanted = tgt_refs[i][...] - (flags_ref[2] + t * tv)
            factor, over, inv, top = column(0), column(1), column(2), stat_cols[i][:, 0:1]
            lane = lane_ids(tc)
            for s in range(0, tv, LANES):
                logits = tile_ref[i][:, s : s + LANES].astype(jnp.int32).astype(f32) * factor
                probs = jnp.exp(logits - top) * over
                grad = (probs - jnp.where(lane == wanted - s, inv, 0.0)).astype(bf16)
                g_refs[i][:, s : s + LANES] = grad
                g_all[i * tc : (i + 1) * tc, s : s + LANES] = grad
        acc[...] += lax.dot_general(
            w_ref[...], g_all[...], (((1,), (1,)), ((), ())), preferred_element_type=f32
        )

        @pl.when(t == tiles - 1)
        def _():
            for i in range(count):
                flipped[...] = jnp.transpose(acc[:, i * tc : (i + 1) * tc])
                for j in range(cols):
                    start = pl.multiple_of((flags_ref[1] ^ j) * tk, tk)
                    part = flipped[pl.ds(start, tk), :].astype(bf16)
                    out_ref = odd_ref if j % 2 else even_ref
                    out_ref[j // 2, i * tk : (i + 1) * tk, :] = part
                info_ref[i] = to_rows(cols_ref[i][:, 3:4])

    code_specs, code_args = [], []
    for own, got in pieces:
        nt = tiles // len(own)
        for use, arrays in ((1, own), (0, got)):
            for h, array in enumerate(arrays):

                def index(t, flags, h=h, use=use, nt=nt):
                    on = flags[0] if use else 1 - flags[0]
                    return (0, jnp.clip(t - h * nt, 0, nt - 1) * on)

                code_specs.append(pl.BlockSpec((tc, tv), index))
                code_args.append(array)
    slots = (cols // 2, count * tk, feats)
    outs = call(
        body,
        (tiles,),
        1,
        code_specs
        + [whole((8, LANES))] * count
        + [whole((tc, 1))] * count
        + [whole((count, 8, LANES)), pl.BlockSpec((feats, tv), lambda t, _: (0, t)), ANY],
        [pl.BlockSpec((tc, tv), lambda t, _: (0, t))] * count
        + [whole(slots), whole(slots), whole((count, 8, LANES))],
        [sds((tc, vocab), bf16)] * count
        + [sds(slots, bf16), sds(slots, bf16), sds((count, 8, LANES), f32)],
        [
            pltpu.VMEM((count, tc, LANES), f32),
            pltpu.VMEM((count, tc, LANES), f32),
            pltpu.VMEM((count, tc, tv), i16),
            pltpu.VMEM((count * tc, tv), bf16),
            pltpu.VMEM((feats, count * tc), f32),
            pltpu.VMEM((tc, feats), f32),
        ],
        (flags, *code_args, *rows8, *target, stats, weight, tok),
    )
    return outs[:count], outs[count], outs[count + 1], outs[count + 2]


def head_product(scaled, grads, tv, part, buffer, tok):
    count = len(scaled)
    tc, feats = scaled[0].shape
    vocab = grads[0].shape[1]
    tiles = vocab // tv // HEAD_PARTS
    given = [] if buffer is None else [buffer]

    def body(*refs):
        xs, gs = refs[:count], refs[count : 2 * count]
        out_ref, small_ref, flipped, g_all = refs[2 * count + 1 + len(given) :]

        @pl.when(pl.program_id(0) == 0)
        def _():
            for i in range(count):
                flipped[:, i * tc : (i + 1) * tc] = jnp.transpose(xs[i][...])
            small_ref[...] = jnp.zeros_like(small_ref)

        for i in range(count):
            g_all[i * tc : (i + 1) * tc, :] = gs[i][...]
        out_ref[...] = jnp.dot(flipped[...], g_all[...], preferred_element_type=f32).astype(bf16)

    return pl.pallas_call(
        body,
        grid=(tiles,),
        in_specs=[whole((tc, feats))] * count
        + [pl.BlockSpec((tc, tv), lambda t: (0, t + part * tiles))] * count
        + [ANY] * (1 + len(given)),
        out_specs=[
            pl.BlockSpec((feats, tv), lambda t: (0, t + part * tiles)),
            whole((8, LANES)),
        ],
        out_shape=[sds((feats, vocab), bf16), sds((8, LANES), f32)],
        scratch_shapes=[
            pltpu.VMEM((feats, count * tc), bf16),
            pltpu.VMEM((count * tc, tv), bf16),
        ],
        input_output_aliases={2 * count + 1: 0} if given else {},
        compiler_params=pltpu.CompilerParams(
            dimension_semantics=("arbitrary",), vmem_limit_bytes=56 << 20
        ),
    )(*scaled, *grads, tok, *given)


def activate(flags, gate, up, cols, tok):
    tokens, width = gate.shape
    rows = tokens // cols
    half = cols // 2

    def body(flags_ref, gate_ref, up_ref, _, out_ref, small_ref):
        value = gate_ref[...].astype(f32)
        out_ref[...] = (value / (1.0 + jnp.exp(-value)) * up_ref[...].astype(f32)).astype(bf16)
        small_ref[...] = jnp.zeros_like(small_ref)

    source = pl.BlockSpec(
        (rows, width), lambda j, flags_ref: (((j % half) * 2 + j // half) ^ flags_ref[1], 0)
    )
    return call(
        body,
        (cols,),
        1,
        [source, source, ANY],
        [pl.BlockSpec((rows, width), lambda j, _: (j, 0)), whole((8, LANES))],
        [sds((tokens, width), bf16), sds((8, LANES), f32)],
        [],
        (flags, gate, up, tok),
    )


def partner(value, mask, axis="col"):
    size = lax.axis_size(axis)
    return lax.ppermute(value, axis, [(i, i ^ mask) for i in range(size)])


def nothing(_):
    pass


def gather_slots(value, meanwhile=nothing):
    size = lax.axis_size("col")
    others = [partner(value, m) for m in range(2, size, 2)]
    meanwhile(value)
    even = jnp.stack([value] + others)
    odd = partner(even, 1)
    meanwhile(even)
    return even, odd


def combine(left, right):
    biggest = jnp.maximum(left[:, 0], right[:, 0])
    left_scale = jnp.exp(left[:, 0] - biggest)
    right_scale = jnp.exp(right[:, 0] - biggest)
    return jnp.stack(
        [
            biggest,
            left[:, 1] * left_scale + right[:, 1] * right_scale,
            left[:, 2] * left_scale + right[:, 2] * right_scale,
            left[:, 3] + right[:, 3],
        ]
        + [left[:, 4]] * 4,
        axis=1,
    )


def over_col(stats):
    step = 1
    while step < lax.axis_size("col"):
        stats = combine(stats, partner(stats, step))
        step *= 2
    return stats


def over_row(value):
    step = 1
    while step < lax.axis_size("row"):
        value = value + partner(value, step, "row")
        step *= 2
    return value


def scatter_slots(even, odd, meanwhile=nothing):
    other = partner(odd, 1)
    meanwhile(odd)
    summed = (even.astype(f32) + other.astype(f32)).astype(bf16)
    others = [partner(summed[i], 2 * i) for i in range(1, even.shape[0])]
    meanwhile(summed)
    total = summed[0].astype(f32)
    for value in others:
        total = total + value.astype(f32)
    return total


def on_device(hidden_state, norm_gain, head_weight, targets, gate_act, up_act):
    tok_col, feats = hidden_state.shape
    vocab_part = head_weight.shape[1]
    cols = lax.axis_size("col")
    rows = lax.axis_size("row")
    half = rows // 2
    row = lax.axis_index("row")
    col = lax.axis_index("col")
    all_feats = feats * rows
    chunks = len(PARTS)
    tk = tok_col // chunks
    tc = tk * cols
    assert tc == LANES and rows in (4, 8, 16) and cols & (cols - 1) == 0
    tv = vocab_part // max(8, *PARTS)
    inner = jnp.where((row == 0) | (row == rows - 1), 0, 1)
    flags = jnp.stack([inner, col, col * vocab_part]).astype(jnp.int32)
    gain = norm_gain[None, :]
    target_chunks = targets.reshape(cols, chunks, tk)
    target_of = [target_chunks[:, k].reshape(tc, 1) for k in range(chunks)]
    tok = norm_gain[:LANES].reshape(1, LANES)

    reduce_pairs = [[(s, s + 1), (rows - 1 - s, rows - 2 - s)] for s in range(half - 1)]
    reduce_pairs.append([(half - 1, half), (half, half - 1)])
    spread_pairs = [
        [(s + 1, s), (rows - 2 - s, rows - 1 - s)] for s in range(half - 2, -1, -1)
    ]

    def move(value, pairs):
        return lax.ppermute(value, "row", pairs)

    even0, odd0 = gather_slots(hidden_state[:tk])
    even1, odd1 = gather_slots(hidden_state[tk:])
    scaled, products, rows8 = logit_parts(flags, even0, odd0, gain, head_weight, 1, tv, tok)
    rows8 = [over_row(rows8[0])]
    current = list(to_codes(products[0], rows8[0], PARTS[0], tok))
    pending = {n: move(current[n], reduce_pairs[0]) for n in range(DEPTH)}
    more, products, more_rows = logit_parts(
        flags, even1, odd1, gain, head_weight, chunks - 1, tv, current[0]
    )
    tok = more[0]
    scaled = list(scaled) + list(more)
    more_rows = over_row(jnp.stack(more_rows))
    rows8 += [more_rows[k] for k in range(chunks - 1)]
    activation = []

    def encode_next(k):
        def run(tok):
            made = to_codes(products[k - 1], rows8[k], PARTS[k], tok)
            current.extend(made)
            return made[0]

        return run

    def run_activation(tok):
        out, tok = activate(flags, gate_act, up_act, cols, tok)
        activation.append(out)
        return tok

    fillers = [encode_next(k) for k in range(1, chunks)] + [run_activation]

    chunk_of = [k for k in range(chunks) for _ in range(PARTS[k])]
    count = len(chunk_of)
    first_of = [chunk_of.index(k) for k in range(chunks)]
    arrived = {}
    final = {}
    stats = {}
    grads, hidden_grads, gathered = [], [], []

    def own_and_got(k):
        span = range(first_of[k], first_of[k] + PARTS[k])
        return [final[p][0] for p in span], [final[p][1] for p in span]

    head = [None]
    done_parts = []

    def head_step(after):
        tok = after if head[0] is None else head[0][1]
        if head[0] is not None:
            after, tok = lax.optimization_barrier((after, tok))
        part = len(done_parts)
        if part < HEAD_PARTS:
            width = min(1024, vocab_part // HEAD_PARTS)
            buffer = None if head[0] is None else head[0][0]
            head[0] = head_product(scaled, grads, width, part, buffer, after)
            done_parts.append(part)

    def finish(group, tok):
        together = over_col(jnp.stack([stats[k] for k in group]))
        grad, even, odd, info = grad_and_feature(
            flags,
            [own_and_got(k) for k in group],
            [rows8[k] for k in group],
            [target_of[k] for k in group],
            together,
            head_weight,
            cols,
            all_feats,
            tv,
            tok,
        )
        grads.extend(grad)
        meanwhile = head_step if group == GROUPS[-1] else nothing
        feature_grad = scatter_slots(even, odd, meanwhile)
        mine = lax.dynamic_slice_in_dim(info[:, 0], col * tk, tk, axis=1).reshape(-1)
        span = slice(group[0] * tk, (group[-1] + 1) * tk)
        wide = hidden_state[span].astype(f32)
        result = (gain * feature_grad - wide * mine[:, None] / all_feats).astype(bf16)
        hidden_grads.append(result)
        gathered.append(gather_slots(result, meanwhile))
        return info

    def add(left, right, tok):
        left, right, _ = lax.optimization_barrier((left, right, tok))
        return left + right

    waiting = list(GROUPS)
    for i in range(count + 2 * half - 1):
        for r in range(half):
            p = i - r
            if not 0 <= p < count:
                continue
            got = pending[p]
            if r == 0 and p + DEPTH < count:
                codes, got = lax.optimization_barrier((current[p + DEPTH], got))
                pending[p + DEPTH] = move(codes, reduce_pairs[0])
            tok = current[p] = add(current[p], got, tok)
            pairs = reduce_pairs[r + 1] if r + 1 < half else spread_pairs[0]
            pending[p] = move(current[p], pairs)
        for q in range(half - 1):
            p = i - half - q
            if not 0 <= p < count:
                continue
            got = pending[p]
            if q + 1 < half - 1:
                s = half - 2 - q
                here = (row == s) | (row == rows - 1 - s)
                current[p] = jnp.where(here, got, current[p])
                pending[p] = move(current[p], spread_pairs[q + 1])
                continue
            final[p] = (current[p], got)
            k = chunk_of[p]
            if p + 1 == count or chunk_of[p + 1] != k:
                own, got = own_and_got(k)
                tok = stats[k] = local_stats(
                    flags, own, got, rows8[k], target_of[k], all_feats, tok
                )
            elif waiting and waiting[0][-1] in stats:
                tok = finish(waiting.pop(0), tok)
        if i >= 1 and fillers:
            tok = fillers.pop(0)(tok)
    for group in waiting:
        tok = finish(group, tok)

    while len(done_parts) < HEAD_PARTS:
        head_step(tok)
    head_grad = head[0][0]
    grad_hidden = jnp.concatenate(hidden_grads)
    gathered = jnp.concatenate([jnp.concatenate(pair) for pair in gathered], axis=1)
    down_sum = lax.dot_general(
        activation[0],
        gathered.reshape(cols * tok_col, feats),
        (((0,), (0,)), ((), ())),
        preferred_element_type=f32,
    )
    return (head_grad, grad_hidden, down_sum.astype(bf16))


def solution(mesh):
    in_specs = (P("col", "row"), P("row"), P("row", "col"), P(), P(None, "col"), P(None, "col"))
    out_specs = (P("row", "col"), P("col", "row"), P("col", "row"))
    return jax.shard_map(
        on_device, mesh=mesh, in_specs=in_specs, out_specs=out_specs, check_vma=False
    )
```
